32 devices in a mesh: gx: 4 (over z), gy: 2 (over y), gz: 4 (over x, core).
Axes of the slice: x: 2, y: 2, z: 4, core: 2. Of those that a mesh axis runs over, the one named last changes fastest.
Arguments:
- positions: float32 [3, 131072], P(None, ('gx', 'gy', 'gz'))
- velocities: float32 [3, 131072], P(None, ('gx', 'gy', 'gz')), may hold values from -6 to 6
- forces_old: float32 [3, 131072], P(None, ('gx', 'gy', 'gz')), may hold values from -6 to 6
- inv_mass: float32 [131072], P(('gx', 'gy', 'gz')), may hold values from 0.25 to 4
- charges: float32 [131072], P(('gx', 'gy', 'gz')), may hold values from -3 to 3
- block_species: int32 [1024], P(('gx', 'gy', 'gz')), may hold values from 0 to 3
- sigma_table: float32 [4], replicated, may hold values from 0.25 to 0.5
- epsilon_table: float32 [4], replicated, may hold values from 0.02 to 0.2
- tower_index: int32 [32, 64], P(('gx', 'gy', 'gz')), may hold values from 0 to 127
- plate_index: int32 [32, 64], P(('gx', 'gy', 'gz')), may hold values from 0 to 287
- tile_counts: int32 [32], P(('gx', 'gy', 'gz')), may hold values from 1 to 64, as said below
- exclusions: int32 [32, 64, 16, 128], P(('gx', 'gy', 'gz')), may hold values from 0 to 255, as said below
- mig_block: int32 [32, 4], P(('gx', 'gy', 'gz')), may hold values from 0 to 31, as said below
- mig_dest: int32 [32, 4], P(('gx', 'gy', 'gz')), may hold values from 0 to 8, as said below
Outputs:
- positions_new: float32 [3, 131072], P(None, ('gx', 'gy', 'gz'))
- velocities_new: float32 [3, 131072], P(None, ('gx', 'gy', 'gz'))
- forces_new: float32 [3, 131072], P(None, ('gx', 'gy', 'gz'))
- arrivals: float32 [6, 32, 8, 512], P(None, ('gx', 'gy', 'gz'))
The draws below stay inside these ranges and needn't reach their ends.
Inputs may be any that keep to these rules, and one draw needn't show every extreme that they name: `tile_counts`: at most 64 for every box, and exactly 64 for some box; slots at or after a box's count carry no weight. `exclusions`: each of the low eight bits marks one excluded atom pair. `mig_block`: the 4 entries of one box are distinct. `mig_dest`: never 4.
All inputs are finite; a program needn't handle non-finite values.
Results may differ from the reference program's by a relative error of at most 0.0003.
Values sent between devices are 32-bit elements; how exact they have to be, the bound alone decides.
A program may use at most 64 MiB of HBM per device.

```python
import math
import jax
import jax.numpy as jnp
from jax import lax

TILE = 128
WORDS = 16
BLOCKS = 32
PAIRS = 64
MIG = 4
KINDS = 4
ATOMS = 131072
N_GX = 4
N_GY = 2
N_GZ = 4
DEVICES = 32


def draw_positions(key, part):
    atoms_box = BLOCKS * TILE
    atom_ids = jnp.arange(atoms_box * DEVICES, dtype=jnp.int32)
    box_ids = atom_ids // atoms_box
    coord_x = (box_ids // (N_GY * N_GZ)).astype(jnp.float32)
    coord_y = (box_ids // N_GZ % N_GY).astype(jnp.float32)
    coord_z = (box_ids % N_GZ).astype(jnp.float32)
    spread = jax.random.uniform(key, (3, atoms_box * DEVICES), jnp.float32)
    layer_height = 1.0 / N_GZ
    return jnp.stack([coord_x + spread[0], coord_y + spread[1], (coord_z + spread[2]) * layer_height], axis=0).astype(jnp.float32)


def draw_tile_counts(key, part):
    first_key, second_key, third_key = jax.random.split(jax.random.fold_in(key, 11), 3)
    left = jax.random.randint(first_key, (DEVICES,), 1, PAIRS + 1)
    right = jax.random.randint(second_key, (DEVICES,), 1, PAIRS + 1)
    counted = jnp.maximum(left * right // PAIRS, 1)
    busiest = jax.random.randint(third_key, (), 0, DEVICES)
    counted = jnp.where(jnp.arange(DEVICES) == busiest, PAIRS, counted)
    return counted.astype(jnp.int32)


def draw_exclusions(key, part):
    first_key, second_key = jax.random.split(jax.random.fold_in(key, 23), 2)
    shape_full = (DEVICES, PAIRS, WORDS, TILE)
    first_bits = jax.random.randint(first_key, shape_full, 0, 256, dtype=jnp.int32)
    second_bits = jax.random.randint(second_key, shape_full, 0, 256, dtype=jnp.int32)
    return jnp.bitwise_and(first_bits, second_bits).astype(jnp.int32)


def draw_mig_block(key, part):
    row_keys = jax.random.split(jax.random.fold_in(key, 37), DEVICES)
    orders = jax.vmap(lambda row_key: jax.random.permutation(row_key, BLOCKS))(row_keys)
    return orders[:, :MIG].astype(jnp.int32)


def draw_mig_dest(key, part):
    picked = jax.random.randint(jax.random.fold_in(key, 41), (DEVICES, MIG), 0, 8)
    return (picked + (picked >= 4).astype(picked.dtype)).astype(jnp.int32)


def plant(values, own_key, least, high):
    dims = values.shape
    place = [jax.random.randint(jax.random.fold_in(own_key, axis), (), 0, dims[axis]) for axis in range(len(dims))]
    values = values.at[tuple(place)].set(least)
    longest = dims.index(max(dims))
    place[longest] = (place[longest] + 1) % dims[longest]
    return values.at[tuple(place)].set(high)


def steps_of(rng, extent, cuts, least, top_value):
    factor_of = 1.0
    for position, blocks in cuts:
        heights = jax.random.uniform(jax.random.fold_in(jax.random.fold_in(rng, 6), position), (blocks,), jnp.float32, least / len(cuts), top_value / len(cuts))
        factor_of = factor_of * jnp.repeat(jnp.exp(heights), extent[position] // blocks).reshape((-1,) + (1,) * (len(extent) - 1 - position))
    return factor_of


def normal_values(key, dims, scale, reach, shards=(), kind=jnp.bfloat16):
    drawn = jax.random.normal(key, dims, jnp.float32) * scale
    if len(shards) > 0:
        drawn = steps_of(key, dims, shards, -0.22, 0.18) * drawn
    return jnp.clip(drawn, min=-reach, max=reach).astype(kind)


def setup_inputs(seed: int = 0) -> dict:
    splits = jax.random.split(jax.random.key(seed), 15)
    return {
        "positions": draw_positions(jax.random.fold_in(splits[14], 71), 0),
        "velocities": normal_values(splits[1], (3, ATOMS), 1.0, 6.0, ((1, 32),), jnp.float32),
        "forces_old": normal_values(splits[2], (3, ATOMS), 1.0, 6.0, ((1, 32),), jnp.float32),
        "inv_mass": jnp.clip(jnp.exp(math.log(4.0) - 2.7725887 * jax.random.uniform(splits[3], (ATOMS,), jnp.float32) ** steps_of(splits[3], (ATOMS,), ((0, 32),), -0.2, 0.2)), 0.25, 4.0),
        "charges": normal_values(splits[4], (ATOMS,), 0.5, 3.0, ((0, 32),), jnp.float32),
        "block_species": plant(jax.random.randint(splits[5], (DEVICES * BLOCKS,), 0, KINDS), jax.random.fold_in(splits[5], 1), 0, KINDS - 1).astype(jnp.int32),
        "sigma_table": jnp.clip(jnp.exp(jax.random.uniform(splits[6], (KINDS,), jnp.float32, math.log(0.25), math.log(0.5))), 0.25, 0.5),
        "epsilon_table": jnp.clip(jnp.exp(jax.random.uniform(splits[7], (KINDS,), jnp.float32, math.log(0.02), math.log(0.2))), 0.02, 0.2),
        "tower_index": plant(jax.random.randint(splits[8], (DEVICES, PAIRS), 0, N_GZ * BLOCKS), jax.random.fold_in(splits[8], 1), 0, (N_GZ * BLOCKS) - 1).astype(jnp.int32),
        "plate_index": plant(jax.random.randint(splits[9], (DEVICES, PAIRS), 0, 9 * BLOCKS), jax.random.fold_in(splits[9], 1), 0, (9 * BLOCKS) - 1).astype(jnp.int32),
        "tile_counts": draw_tile_counts(jax.random.fold_in(splits[14], 71), 0),
        "exclusions": draw_exclusions(jax.random.fold_in(splits[14], 71), 0),
        "mig_block": draw_mig_block(jax.random.fold_in(splits[14], 71), 0),
        "mig_dest": draw_mig_dest(jax.random.fold_in(splits[14], 71), 0),
    }


time_step = 0.2
soft_core = 0.09
cutoff_sq = 1.44
coulomb_k = 0.5

def tile_terms(tower_rows, plate_rows, mask_words, length_x, length_y):
    tile_width = tower_rows.shape[1]
    raw = tower_rows[0:3, :, None] - plate_rows[0:3, None, :]
    image_x = raw[0] - length_x * jnp.floor(raw[0] / length_x + 0.5)
    image_y = raw[1] - length_y * jnp.floor(raw[1] / length_y + 0.5)
    offsets = jnp.stack([image_x, image_y, raw[2]], axis=0)
    distance_sq = lax.optimization_barrier(jnp.sum(offsets * offsets, axis=0))
    inverse = 1.0 / (distance_sq + soft_core)
    sigma_pair = 0.5 * (tower_rows[4][:, None] + plate_rows[4][None, :])
    ratio_pair = sigma_pair * sigma_pair * inverse
    ratio_cube = ratio_pair * ratio_pair * ratio_pair
    depth_pair = tower_rows[5][:, None] * plate_rows[5][None, :]
    charge_term = coulomb_k * tower_rows[3][:, None] * plate_rows[3][None, :] * jnp.sqrt(inverse)
    falloff = 1.0 - distance_sq / cutoff_sq
    switch = jnp.where(distance_sq < cutoff_sq, falloff * falloff, 0.0)
    spread = jnp.repeat(mask_words.T, 8, axis=1)
    shifts = jnp.arange(tile_width, dtype=jnp.int32) % 8
    excluded = jnp.bitwise_and(jnp.right_shift(spread, shifts[None, :]), 1)
    kept_pairs = (1 - excluded).astype(jnp.float32)
    strength = (depth_pair * (12.0 * ratio_cube * ratio_cube - 6.0 * ratio_cube) + charge_term) * inverse * switch * kept_pairs
    weighted = strength[None] * offsets
    return (lax.optimization_barrier(jnp.sum(weighted, axis=2)), -lax.optimization_barrier(jnp.sum(weighted, axis=1)))

def box_number(coord_x, coord_y, coord_z):
    return (coord_x * N_GY + coord_y) * N_GZ + coord_z

def reference(positions, velocities, forces_old, inv_mass, charges, block_species, sigma_table, epsilon_table, tower_index, plate_index, tile_counts, exclusions, mig_block, mig_dest):
    half_kick = velocities + 0.5 * time_step * forces_old * inv_mass[None, :]
    moved = positions + time_step * half_kick
    sigma_atom = jnp.repeat(sigma_table[block_species], TILE)
    depth_atom = jnp.repeat(jnp.sqrt(epsilon_table)[block_species], TILE)
    features = jnp.concatenate([moved, charges[None, :], sigma_atom[None, :], depth_atom[None, :]], axis=0)
    block_rows = features.reshape(6, DEVICES * BLOCKS, TILE)
    pair_slots = jnp.arange(PAIRS, dtype=jnp.int32)
    length_x = float(N_GX)
    length_y = float(N_GY)

    def pair_terms(tower_rows, plate_rows, mask_words):
        return tile_terms(tower_rows, plate_rows, mask_words, length_x, length_y)

    def one_box(totals, inputs):
        box_index, tower_list, plate_list, pair_count, mask_list = inputs
        coord_x = box_index // (N_GY * N_GZ)
        coord_y = box_index // N_GZ % N_GY
        coord_z = box_index % N_GZ
        tower_ids = box_number(coord_x, coord_y, tower_list // BLOCKS) * BLOCKS + tower_list % BLOCKS
        neighbour = plate_list // BLOCKS
        plate_ids = box_number((coord_x + neighbour // 3 - 1) % N_GX, (coord_y + neighbour % 3 - 1) % N_GY, coord_z) * BLOCKS + plate_list % BLOCKS
        tower_tiles = jnp.take(block_rows, tower_ids, axis=1)
        plate_tiles = jnp.take(block_rows, plate_ids, axis=1)
        on_tower, on_plate = jax.vmap(pair_terms, in_axes=(1, 1, 0), out_axes=1)(tower_tiles, plate_tiles, mask_list)
        listed = (pair_slots < pair_count).astype(jnp.float32)[None, :, None]
        totals = totals.at[:, tower_ids].add(on_tower * listed)
        totals = totals.at[:, plate_ids].add(on_plate * listed)
        return (totals, None)
    boxes = jnp.arange(DEVICES, dtype=jnp.int32)
    start = jnp.zeros((3, DEVICES * BLOCKS, TILE), jnp.float32)
    totals = lax.scan(one_box, start, (boxes, tower_index, plate_index, tile_counts, exclusions))[0]
    forces_new = totals.reshape(3, DEVICES * BLOCKS * TILE)
    velocity_full = half_kick + 0.5 * time_step * forces_new * inv_mass[None, :]
    departed = jnp.zeros((DEVICES, BLOCKS), jnp.float32).at[boxes[:, None], mig_block].set(1.0)
    staying = jnp.repeat((1.0 - departed).reshape(-1), TILE)[None, :]
    positions_new = moved * staying
    velocities_new = velocity_full * staying
    state = jnp.concatenate([moved, velocity_full], axis=0).reshape(6, DEVICES * BLOCKS, TILE)
    shift_x = jnp.array([-1, -1, -1, 0, 0, 1, 1, 1], dtype=jnp.int32)
    shift_y = jnp.array([-1, 0, 1, -1, 1, -1, 0, 1], dtype=jnp.int32)
    coord_x = boxes // (N_GY * N_GZ)
    coord_y = boxes // N_GZ % N_GY
    coord_z = boxes % N_GZ
    sources = box_number((coord_x[:, None] + shift_x[None, :]) % N_GX, (coord_y[:, None] + shift_y[None, :]) % N_GY, coord_z[:, None])
    source_ids = sources[:, :, None] * BLOCKS + mig_block[sources]
    wanted = (mig_dest[sources] == ((1 - shift_x) * 3 + (1 - shift_y))[None, :, None]).astype(jnp.float32)
    picked = jnp.take(state, source_ids.reshape(-1), axis=1).reshape(6, DEVICES, 8, MIG, TILE)
    arrivals = (picked * wanted[None, :, :, :, None]).reshape(6, DEVICES, 8, MIG * TILE)
    return (positions_new, velocities_new, forces_new, arrivals)
```

```python
import functools
import jax
import jax.numpy as jnp
from jax import lax
from jax.experimental import pallas as pl
from jax.experimental.pallas import tpu as pltpu
from jax.sharding import PartitionSpec as P

time_step = 0.2
soft_core = 0.09
cutoff_sq = 1.44
coulomb_k = 0.5
MESH = pl.DeviceIdType.MESH
source_offsets = ((-1, -1), (-1, 0), (-1, 1), (0, -1), (0, 1), (1, -1), (1, 0), (1, 1))
GROUP = 2


class Slots:
    def __init__(self, nx, ny, nz):
        self.nx, self.ny, self.nz = nx, ny, nz
        self.offsets = [(0, 0, 0)] + [(0, 0, k) for k in range(1, nz)]
        self.cell = {(0, 0): 0}
        for da in range(-1, 2):
            for db in range(-1, 2):
                key = (da % nx, db % ny)
                if key not in self.cell:
                    self.cell[key] = len(self.offsets)
                    self.offsets.append((key[0], key[1], 0))
        self.count = len(self.offsets)

    def cell_slot(self, da, db):
        return self.cell[(da % self.nx, db % self.ny)]

    def opposite(self, slot):
        dx, dy, dz = self.offsets[slot]
        if dz:
            return (self.nz - dz) % self.nz
        return self.cell_slot(-dx, -dy)

    def device(self, slot):
        dx, dy, dz = self.offsets[slot]
        return (
            lax.rem(lax.axis_index("gx") + dx, self.nx),
            lax.rem(lax.axis_index("gy") + dy, self.ny),
            lax.rem(lax.axis_index("gz") + dz, self.nz),
        )


def greet(slots):
    barrier = pltpu.get_barrier_semaphore()
    for s in range(1, slots.count):
        pl.semaphore_signal(barrier, inc=1, device_id=slots.device(s), device_id_type=MESH)
    pl.semaphore_wait(barrier, slots.count - 1)


def gather_kernel(
    slots, sigma_ref, eps_ref, pos, vel, fold, mass, charge, species, feats, kinds, send, recv, send2, recv2
):
    blocks = species.shape[1]
    half = vel[...] + 0.5 * time_step * fold[...] * mass[...]
    feats[0, 0:3, :] = pos[...] + time_step * half
    feats[0, 3:4, :] = charge[...]
    which = species[...]
    sigma = jnp.zeros((1, blocks), jnp.float32)
    eps = jnp.zeros((1, blocks), jnp.float32)
    for k in range(sigma_ref.shape[0]):
        sigma = jnp.where(which == k, sigma_ref[k], sigma)
        eps = jnp.where(which == k, eps_ref[k], eps)
    kinds[0] = jnp.zeros(kinds.shape[1:], jnp.float32)
    kinds[0, 0:1, 0:blocks] = sigma
    kinds[0, 1:2, 0:blocks] = jnp.sqrt(eps)
    greet(slots)
    copies = []
    for s in range(1, slots.count):
        there = slots.opposite(s)
        for ref, ss, rs in ((kinds, send2, recv2), (feats, send, recv)):
            copy = pltpu.make_async_remote_copy(
                src_ref=ref.at[0],
                dst_ref=ref.at[there],
                send_sem=ss.at[s],
                recv_sem=rs.at[there],
                device_id=slots.device(s),
                device_id_type=MESH,
            )
            copy.start()
            copies.append(copy)
    for copy in copies:
        copy.wait()


def pair_kernel(slots, blocks, tower, plate, counts, kinds, feats, excl, acc, cell_table):
    width = excl.shape[-1]
    words = excl.shape[2]
    lanes8 = width // words
    nx, ny, nz = slots.nx, slots.ny, slots.nz
    lx, ly = float(nx), float(ny)
    my_layer = lax.axis_index("gz")
    for o in range(9):
        cell_table[o] = slots.cell_slot(o // 3 - 1, o % 3 - 1)
    acc[...] = jnp.zeros(acc.shape, acc.dtype)
    count = counts[0]
    bit = jnp.left_shift(1, lax.broadcasted_iota(jnp.int32, (lanes8, width), 0))
    lane = lax.broadcasted_iota(jnp.int32, (lanes8, width), 1)
    shift_h = soft_core / (lx * lx)
    edge = (cutoff_sq + soft_core) / (lx * lx)
    ratio = (ly / lx) ** 2
    scale = lx * lx / (cutoff_sq * cutoff_sq)

    def one_slot(k, listed):
        t = tower[0, k]
        p = plate[0, k]
        t_slot = lax.rem(t // blocks - my_layer + nz, nz)
        p_slot = cell_table[p // blocks]
        t_block = lax.rem(t, blocks)
        p_block = lax.rem(p, blocks)
        sig = 0.5 * (kinds[t_slot, 0, t_block] + kinds[p_slot, 0, p_block])
        depth = kinds[t_slot, 1, t_block] * kinds[p_slot, 1, p_block]
        sig2 = sig * sig
        sig6 = sig2 * sig2 * sig2
        live = jnp.where(listed, jnp.float32(1.0), jnp.float32(0.0))
        att = (6.0 * scale / lx**6) * depth * sig6 * live
        rep = (12.0 * scale / lx**12) * depth * sig6 * sig6 * live
        t_at = pl.ds(pl.multiple_of(t_block * width, width), width)
        p_at = pl.ds(pl.multiple_of(p_block * width, width), width)
        rows = feats[t_slot, :, t_at]
        prow = feats[p_slot, :, p_at]
        full = (lanes8, width)
        tx = jnp.broadcast_to(rows[0:1] * (1.0 / lx), full)
        ty = jnp.broadcast_to(rows[1:2] * (1.0 / ly), full)
        tz = jnp.broadcast_to(rows[2:3] * (1.0 / lx), full)
        tq = jnp.broadcast_to(rows[3:4] * (coulomb_k * scale / lx) * live, full)
        cols = jnp.concatenate(
            [prow[0:1] * (1.0 / lx), prow[1:2] * (1.0 / ly), prow[2:3] * (1.0 / lx), prow[3:4]] * 2, axis=0
        ).T
        sx = sy = sz = None
        back = []
        for w in range(words):
            piece = cols[w * lanes8 : (w + 1) * lanes8]
            dx = tx - piece[:, 0:1]
            dy = ty - piece[:, 1:2]
            dz = tz - piece[:, 2:3]
            dx = dx - jnp.floor(dx + 0.5)
            dy = dy - jnp.floor(dy + 0.5)
            h = (dx * dx + dz * dz) + (ratio * (dy * dy) + shift_h)
            q = lax.rsqrt(h)
            f = jnp.maximum(edge - h, 0.0)
            s = q * q
            s3 = s * s * s
            g = f * f * s
            e = s3 * (rep * s3 - att) + (tq * piece[:, 3:4]) * q
            c = jnp.where((excl[0, k, w : w + 1, :] & bit) == 0, e * g, 0.0)
            fx, fy, fz = c * dx, c * dy, c * dz
            sx = fx if sx is None else sx + fx
            sy = fy if sy is None else sy + fy
            sz = fz if sz is None else sz + fz
            rx = jnp.sum(fx, axis=1, keepdims=True)
            ry = jnp.sum(fy, axis=1, keepdims=True)
            rz = jnp.sum(fz, axis=1, keepdims=True)
            back.append(jnp.where(lane == 0, rx, jnp.where(lane == 1, ry, rz)))
        on_plate = jnp.concatenate(back, axis=0).T
        lengths = (lx, ly, lx)
        for r, total in enumerate((sx, sy, sz)):
            row = jnp.sum(total, axis=0, keepdims=True) * lengths[r]
            acc[t_slot, r : r + 1, t_at] += row
        for r in range(3):
            acc[p_slot, r : r + 1, p_at] -= on_plate[r : r + 1] * lengths[r]

    def step(i, carry):
        for g in range(GROUP):
            k = i * GROUP + g
            safe = jnp.minimum(k, tower.shape[1] - 1)
            one_slot(safe, k < count)
        return carry

    lax.fori_loop(0, (count + GROUP - 1) // GROUP, step, 0)


def return_kernel(
    slots, blocks, mig_block, mig_dest, acc, pos, vel, fold, mass,
    pos_out, vel_out, force_out, arrive, landed, state, outgoing, arrived, send, recv, send2, recv2,
):
    atoms = pos.shape[1]
    width = atoms // blocks
    leaving = mig_block.shape[1]
    greet(slots)
    copies = []
    for s in range(1, slots.count):
        there = slots.opposite(s)
        copy = pltpu.make_async_remote_copy(
            src_ref=acc.at[s],
            dst_ref=landed.at[there],
            send_sem=send.at[s],
            recv_sem=recv.at[there],
            device_id=slots.device(s),
            device_id_type=MESH,
        )
        copy.start()
        copies.append(copy)
    half = vel[...] + 0.5 * time_step * fold[...] * mass[...]
    moved = pos[...] + time_step * half
    state[0:3, :] = moved
    state[6:8, :] = jnp.zeros((2, atoms), jnp.float32)
    block_of = lax.broadcasted_iota(jnp.int32, (3, atoms), 1) // width
    gone = block_of == mig_block[0, 0]
    for q in range(1, leaving):
        gone = gone | (block_of == mig_block[0, q])
    stay = jnp.where(gone, 0.0, 1.0)
    pos_out[...] = moved * stay
    for copy in copies:
        copy.wait()
    force = acc[0, 0:3, :]
    for s in range(1, slots.count):
        force = force + landed[s, 0:3, :]
    full = half + 0.5 * time_step * force * mass[...]
    state[3:6, :] = full
    for q in range(leaving):
        chosen = jnp.full((8, width), mig_block[0, q], jnp.int32)
        picked = jnp.zeros((8, width), jnp.float32)
        for b in range(blocks):
            picked = jnp.where(chosen == b, state[:, b * width : (b + 1) * width], picked)
        outgoing[0:6, q * width : (q + 1) * width] = picked[0:6]
        outgoing[6:8, q * width : (q + 1) * width] = jnp.full((2, width), mig_dest[0, q], jnp.int32).astype(
            jnp.float32
        )
    force_out[...] = force
    vel_out[...] = full * stay
    near = sorted({slots.cell_slot(a, b) for a, b in source_offsets} - {0})
    copies = []
    for s in near:
        there = slots.opposite(s)
        copy = pltpu.make_async_remote_copy(
            src_ref=outgoing,
            dst_ref=arrived.at[there],
            send_sem=send2.at[s],
            recv_sem=recv2.at[there],
            device_id=slots.device(s),
            device_id_type=MESH,
        )
        copy.start()
        copies.append(copy)
    for copy in copies:
        copy.wait()
    for i, (a, b) in enumerate(source_offsets):
        slot = slots.cell_slot(a, b)
        got = outgoing[...] if slot == 0 else arrived[slot]
        wanted = float((1 - a) * 3 + (1 - b))
        arrive[:, 0, i, :] = jnp.where(got[6:7] == wanted, got[0:6], 0.0)


def local(
    slots, positions, velocities, forces_old, inv_mass, charges, block_species, sigma_table, epsilon_table,
    tower_index, plate_index, tile_counts, exclusions, mig_block, mig_dest,
):
    atoms = positions.shape[1]
    blocks = block_species.shape[0]
    width = atoms // blocks
    n = slots.count
    leaving = mig_block.shape[1]
    vmem = pl.BlockSpec(memory_space=pltpu.VMEM)
    smem = pl.BlockSpec(memory_space=pltpu.SMEM)
    mass = inv_mass[None, :]
    f32 = jnp.float32
    lanes = max(width, blocks)
    sems = pltpu.SemaphoreType.DMA((n,))
    feats, kinds = pl.pallas_call(
        functools.partial(gather_kernel, slots),
        out_shape=(jax.ShapeDtypeStruct((n, 4, atoms), f32), jax.ShapeDtypeStruct((n, 2, lanes), f32)),
        in_specs=[smem, smem] + [vmem] * 6,
        out_specs=(vmem, vmem),
        scratch_shapes=[sems] * 4,
        compiler_params=pltpu.CompilerParams(collective_id=0, has_side_effects=True),
        name="gather_features",
    )(sigma_table, epsilon_table, positions, velocities, forces_old, mass, charges[None, :], block_species[None, :])
    acc = pl.pallas_call(
        functools.partial(pair_kernel, slots, blocks),
        out_shape=jax.ShapeDtypeStruct((n, 4, atoms), f32),
        in_specs=[smem] * 4 + [vmem] * 2,
        out_specs=vmem,
        scratch_shapes=[pltpu.SMEM((9,), jnp.int32)],
        name="pair_forces",
    )(tower_index, plate_index, tile_counts, kinds, feats, exclusions)
    rows = jax.ShapeDtypeStruct((3, atoms), f32)
    return pl.pallas_call(
        functools.partial(return_kernel, slots, blocks),
        out_shape=(rows, rows, rows, jax.ShapeDtypeStruct((6, 1, len(source_offsets), leaving * width), f32)),
        in_specs=[smem] * 2 + [vmem] * 5,
        out_specs=(vmem,) * 4,
        scratch_shapes=[
            pltpu.VMEM((n, 4, atoms), f32),
            pltpu.VMEM((8, atoms), f32),
            pltpu.VMEM((8, leaving * width), f32),
            pltpu.VMEM((n, 8, leaving * width), f32),
        ]
        + [sems] * 4,
        compiler_params=pltpu.CompilerParams(collective_id=1, has_side_effects=True),
        name="return_forces",
    )(mig_block, mig_dest, acc, positions, velocities, forces_old, mass)


def solution(mesh):
    cells = ("gx", "gy", "gz")
    slots = Slots(mesh.shape["gx"], mesh.shape["gy"], mesh.shape["gz"])
    row = P(None, cells)
    flat = P(cells)
    pair = P(cells, None)
    in_specs = (
        row, row, row, flat, flat, flat, P(), P(), pair, pair, flat, P(cells, None, None, None), pair, pair,
    )
    out_specs = (row, row, row, P(None, cells, None, None))
    return jax.shard_map(
        functools.partial(local, slots), mesh=mesh, in_specs=in_specs, out_specs=out_specs, check_vma=False
    )
```

```python
import functools
import jax
import jax.numpy as jnp
from jax import lax
from jax.experimental import pallas as pl
from jax.experimental.pallas import tpu as pltpu
from jax.sharding import PartitionSpec as P

time_step = 0.2
soft_core = 0.09
cutoff_sq = 1.44
coulomb_k = 0.5
MESH = pl.DeviceIdType.MESH
source_offsets = ((-1, -1), (-1, 0), (-1, 1), (0, -1), (0, 1), (1, -1), (1, 0), (1, 1))
GROUP = 2


class Slots:
    def __init__(self, nx, ny, nz):
        self.nx, self.ny, self.nz = nx, ny, nz
        self.offsets = [(0, 0, 0)] + [(0, 0, k) for k in range(1, nz)]
        self.cell = {(0, 0): 0}
        for da in range(-1, 2):
            for db in range(-1, 2):
                key = (da % nx, db % ny)
                if key not in self.cell:
                    self.cell[key] = len(self.offsets)
                    self.offsets.append((key[0], key[1], 0))
        self.count = len(self.offsets)

    def cell_slot(self, da, db):
        return self.cell[(da % self.nx, db % self.ny)]

    def opposite(self, slot):
        dx, dy, dz = self.offsets[slot]
        if dz:
            return (self.nz - dz) % self.nz
        return self.cell_slot(-dx, -dy)

    def device(self, slot):
        dx, dy, dz = self.offsets[slot]
        return (
            lax.rem(lax.axis_index("gx") + dx, self.nx),
            lax.rem(lax.axis_index("gy") + dy, self.ny),
            lax.rem(lax.axis_index("gz") + dz, self.nz),
        )


def greet(slots):
    barrier = pltpu.get_barrier_semaphore()
    for s in range(1, slots.count):
        pl.semaphore_signal(barrier, inc=1, device_id=slots.device(s), device_id_type=MESH)
    pl.semaphore_wait(barrier, slots.count - 1)


def gather_kernel(
    slots, sigma_ref, eps_ref, pos, vel, fold, mass, charge, species, feats, kinds, send, recv, send2, recv2
):
    blocks = species.shape[1]
    half = vel[...] + 0.5 * time_step * fold[...] * mass[...]
    feats[0, 0:3, :] = pos[...] + time_step * half
    feats[0, 3:4, :] = charge[...]
    which = species[...]
    sigma = jnp.zeros((1, blocks), jnp.float32)
    eps = jnp.zeros((1, blocks), jnp.float32)
    for k in range(sigma_ref.shape[0]):
        sigma = jnp.where(which == k, sigma_ref[k], sigma)
        eps = jnp.where(which == k, eps_ref[k], eps)
    kinds[0] = jnp.zeros(kinds.shape[1:], jnp.float32)
    kinds[0, 0:1, 0:blocks] = sigma
    kinds[0, 1:2, 0:blocks] = jnp.sqrt(eps)
    greet(slots)
    copies = []
    for s in range(1, slots.count):
        there = slots.opposite(s)
        for ref, ss, rs in ((kinds, send2, recv2), (feats, send, recv)):
            copy = pltpu.make_async_remote_copy(
                src_ref=ref.at[0],
                dst_ref=ref.at[there],
                send_sem=ss.at[s],
                recv_sem=rs.at[there],
                device_id=slots.device(s),
                device_id_type=MESH,
            )
            copy.start()
            copies.append(copy)
    for copy in copies:
        copy.wait()


def pair_kernel(slots, blocks, tower, plate, counts, kinds, feats, excl, acc, cell_table):
    width = excl.shape[-1]
    words = excl.shape[2]
    lanes8 = width // words
    nx, ny, nz = slots.nx, slots.ny, slots.nz
    lx, ly = float(nx), float(ny)
    my_layer = lax.axis_index("gz")
    for o in range(9):
        cell_table[o] = slots.cell_slot(o // 3 - 1, o % 3 - 1)
    acc[...] = jnp.zeros(acc.shape, acc.dtype)
    count = counts[0]
    bit = jnp.left_shift(1, lax.broadcasted_iota(jnp.int32, (lanes8, width), 0))
    lane = lax.broadcasted_iota(jnp.int32, (lanes8, width), 1)
    shift_h = soft_core / (lx * lx)
    edge = (cutoff_sq + soft_core) / (lx * lx)
    ratio = (ly / lx) ** 2
    scale = lx * lx / (cutoff_sq * cutoff_sq)

    sub = lax.broadcasted_iota(jnp.int32, (8, width), 0)

    def three(row):
        value = jnp.broadcast_to(row, (8, width))
        high = value.astype(jnp.bfloat16).astype(jnp.float32)
        rest = value - high
        mid = rest.astype(jnp.bfloat16).astype(jnp.float32)
        return [high, mid, rest - mid]

    def by_row(values):
        made = jnp.zeros((8, width), jnp.float32)
        for i, v in enumerate(values):
            made = jnp.where(sub == i, v, made)
        return made

    def one_slot(k, listed):
        t = tower[0, k]
        p = plate[0, k]
        t_slot = lax.rem(t // blocks - my_layer + nz, nz)
        p_slot = cell_table[p // blocks]
        t_block = lax.rem(t, blocks)
        p_block = lax.rem(p, blocks)
        sig = 0.5 * (kinds[t_slot, 0, t_block] + kinds[p_slot, 0, p_block])
        depth = kinds[t_slot, 1, t_block] * kinds[p_slot, 1, p_block]
        sig2 = sig * sig
        sig6 = sig2 * sig2 * sig2
        live = jnp.where(listed, jnp.float32(1.0), jnp.float32(0.0))
        att = (6.0 * scale / lx**6) * depth * sig6 * live
        rep = (12.0 * scale / lx**12) * depth * sig6 * sig6 * live
        t_at = pl.ds(pl.multiple_of(t_block * width, width), width)
        p_at = pl.ds(pl.multiple_of(p_block * width, width), width)
        rows = feats[t_slot, :, t_at]
        prow = feats[p_slot, :, p_at]
        units = (1.0 / lx, 1.0 / ly, 1.0 / lx)
        left, right = [], []
        for r in range(3):
            left.append(by_row([-v for v in three(prow[r : r + 1] * units[r])] + [1.0, 1.0, 1.0]))
            right.append(by_row([1.0, 1.0, 1.0] + three(rows[r : r + 1] * units[r])))
        high, mid, low = three(prow[3:4])
        left.append(by_row([high, high, high, mid, mid, low]))
        high, mid, low = three(rows[3:4] * (coulomb_k * scale / lx) * live)
        right.append(by_row([high, mid, low, high, mid, high]))
        zero = jnp.zeros((8, width), jnp.float32)
        left = jnp.concatenate(left, axis=0).T.astype(jnp.bfloat16)
        right = jnp.concatenate(
            [jnp.concatenate([right[r] if r == m else zero for r in range(4)], axis=0) for m in range(4)], axis=1
        ).astype(jnp.bfloat16)
        made = jnp.dot(left, right, preferred_element_type=jnp.float32)
        sx = sy = sz = None
        back = []
        for w in range(words):
            piece = made[w * lanes8 : (w + 1) * lanes8]
            dx = piece[:, 0:width]
            dy = piece[:, width : 2 * width]
            dz = piece[:, 2 * width : 3 * width]
            dx = dx - jnp.floor(dx + 0.5)
            dy = dy - jnp.floor(dy + 0.5)
            h = (dx * dx + dz * dz) + (ratio * (dy * dy) + shift_h)
            q = lax.rsqrt(h)
            f = jnp.maximum(edge - h, 0.0)
            s = q * q
            s3 = s * s * s
            g = f * f * s
            e = s3 * (rep * s3 - att) + piece[:, 3 * width :] * q
            c = jnp.where((excl[0, k, w : w + 1, :] & bit) == 0, e * g, 0.0)
            fx, fy, fz = c * dx, c * dy, c * dz
            sx = fx if sx is None else sx + fx
            sy = fy if sy is None else sy + fy
            sz = fz if sz is None else sz + fz
            rx = jnp.sum(fx, axis=1, keepdims=True)
            ry = jnp.sum(fy, axis=1, keepdims=True)
            rz = jnp.sum(fz, axis=1, keepdims=True)
            back.append(jnp.where(lane == 0, rx, jnp.where(lane == 1, ry, rz)))
        on_plate = jnp.concatenate(back, axis=0).T
        lengths = (lx, ly, lx)
        for r, total in enumerate((sx, sy, sz)):
            row = jnp.sum(total, axis=0, keepdims=True) * lengths[r]
            acc[t_slot, r : r + 1, t_at] += row
        for r in range(3):
            acc[p_slot, r : r + 1, p_at] -= on_plate[r : r + 1] * lengths[r]

    def step(i, carry):
        for g in range(GROUP):
            k = i * GROUP + g
            safe = jnp.minimum(k, tower.shape[1] - 1)
            one_slot(safe, k < count)
        return carry

    lax.fori_loop(0, (count + GROUP - 1) // GROUP, step, 0)


def return_kernel(
    slots, blocks, mig_block, mig_dest, acc, pos, vel, fold, mass,
    pos_out, vel_out, force_out, arrive, landed, state, outgoing, arrived, send, recv, send2, recv2,
):
    atoms = pos.shape[1]
    width = atoms // blocks
    leaving = mig_block.shape[1]
    greet(slots)
    copies = []
    for s in range(1, slots.count):
        there = slots.opposite(s)
        copy = pltpu.make_async_remote_copy(
            src_ref=acc.at[s],
            dst_ref=landed.at[there],
            send_sem=send.at[s],
            recv_sem=recv.at[there],
            device_id=slots.device(s),
            device_id_type=MESH,
        )
        copy.start()
        copies.append(copy)
    half = vel[...] + 0.5 * time_step * fold[...] * mass[...]
    moved = pos[...] + time_step * half
    state[0:3, :] = moved
    state[6:8, :] = jnp.zeros((2, atoms), jnp.float32)
    block_of = lax.broadcasted_iota(jnp.int32, (3, atoms), 1) // width
    gone = block_of == mig_block[0, 0]
    for q in range(1, leaving):
        gone = gone | (block_of == mig_block[0, q])
    stay = jnp.where(gone, 0.0, 1.0)
    pos_out[...] = moved * stay
    for copy in copies:
        copy.wait()
    force = acc[0, 0:3, :]
    for s in range(1, slots.count):
        force = force + landed[s, 0:3, :]
    full = half + 0.5 * time_step * force * mass[...]
    state[3:6, :] = full
    for q in range(leaving):
        chosen = jnp.full((8, width), mig_block[0, q], jnp.int32)
        picked = jnp.zeros((8, width), jnp.float32)
        for b in range(blocks):
            picked = jnp.where(chosen == b, state[:, b * width : (b + 1) * width], picked)
        outgoing[0:6, q * width : (q + 1) * width] = picked[0:6]
        outgoing[6:8, q * width : (q + 1) * width] = jnp.full((2, width), mig_dest[0, q], jnp.int32).astype(
            jnp.float32
        )
    force_out[...] = force
    vel_out[...] = full * stay
    near = sorted({slots.cell_slot(a, b) for a, b in source_offsets} - {0})
    copies = []
    for s in near:
        there = slots.opposite(s)
        copy = pltpu.make_async_remote_copy(
            src_ref=outgoing,
            dst_ref=arrived.at[there],
            send_sem=send2.at[s],
            recv_sem=recv2.at[there],
            device_id=slots.device(s),
            device_id_type=MESH,
        )
        copy.start()
        copies.append(copy)
    for copy in copies:
        copy.wait()
    for i, (a, b) in enumerate(source_offsets):
        slot = slots.cell_slot(a, b)
        got = outgoing[...] if slot == 0 else arrived[slot]
        wanted = float((1 - a) * 3 + (1 - b))
        arrive[:, 0, i, :] = jnp.where(got[6:7] == wanted, got[0:6], 0.0)


def local(
    slots, positions, velocities, forces_old, inv_mass, charges, block_species, sigma_table, epsilon_table,
    tower_index, plate_index, tile_counts, exclusions, mig_block, mig_dest,
):
    atoms = positions.shape[1]
    blocks = block_species.shape[0]
    width = atoms // blocks
    n = slots.count
    leaving = mig_block.shape[1]
    vmem = pl.BlockSpec(memory_space=pltpu.VMEM)
    smem = pl.BlockSpec(memory_space=pltpu.SMEM)
    mass = inv_mass[None, :]
    f32 = jnp.float32
    lanes = max(width, blocks)
    sems = pltpu.SemaphoreType.DMA((n,))
    feats, kinds = pl.pallas_call(
        functools.partial(gather_kernel, slots),
        out_shape=(jax.ShapeDtypeStruct((n, 4, atoms), f32), jax.ShapeDtypeStruct((n, 2, lanes), f32)),
        in_specs=[smem, smem] + [vmem] * 6,
        out_specs=(vmem, vmem),
        scratch_shapes=[sems] * 4,
        compiler_params=pltpu.CompilerParams(collective_id=0, has_side_effects=True),
        name="gather_features",
    )(sigma_table, epsilon_table, positions, velocities, forces_old, mass, charges[None, :], block_species[None, :])
    acc = pl.pallas_call(
        functools.partial(pair_kernel, slots, blocks),
        out_shape=jax.ShapeDtypeStruct((n, 4, atoms), f32),
        in_specs=[smem] * 4 + [vmem] * 2,
        out_specs=vmem,
        scratch_shapes=[pltpu.SMEM((9,), jnp.int32)],
        name="pair_forces",
    )(tower_index, plate_index, tile_counts, kinds, feats, exclusions)
    rows = jax.ShapeDtypeStruct((3, atoms), f32)
    return pl.pallas_call(
        functools.partial(return_kernel, slots, blocks),
        out_shape=(rows, rows, rows, jax.ShapeDtypeStruct((6, 1, len(source_offsets), leaving * width), f32)),
        in_specs=[smem] * 2 + [vmem] * 5,
        out_specs=(vmem,) * 4,
        scratch_shapes=[
            pltpu.VMEM((n, 4, atoms), f32),
            pltpu.VMEM((8, atoms), f32),
            pltpu.VMEM((8, leaving * width), f32),
            pltpu.VMEM((n, 8, leaving * width), f32),
        ]
        + [sems] * 4,
        compiler_params=pltpu.CompilerParams(collective_id=1, has_side_effects=True),
        name="return_forces",
    )(mig_block, mig_dest, acc, positions, velocities, forces_old, mass)


def solution(mesh):
    cells = ("gx", "gy", "gz")
    slots = Slots(mesh.shape["gx"], mesh.shape["gy"], mesh.shape["gz"])
    row = P(None, cells)
    flat = P(cells)
    pair = P(cells, None)
    in_specs = (
        row, row, row, flat, flat, flat, P(), P(), pair, pair, flat, P(cells, None, None, None), pair, pair,
    )
    out_specs = (row, row, row, P(None, cells, None, None))
    return jax.shard_map(
        functools.partial(local, slots), mesh=mesh, in_specs=in_specs, out_specs=out_specs, check_vma=False
    )
```

```python
import functools
import jax
import jax.numpy as jnp
from jax import lax
from jax.experimental import pallas as pl
from jax.experimental.pallas import tpu as pltpu
from jax.sharding import PartitionSpec as P

time_step = 0.2
soft_core = 0.09
cutoff_sq = 1.44
coulomb_k = 0.5
MESH = pl.DeviceIdType.MESH
source_offsets = ((-1, -1), (-1, 0), (-1, 1), (0, -1), (0, 1), (1, -1), (1, 0), (1, 1))


class Slots:
    def __init__(self, nx, ny, nz):
        self.nx, self.ny, self.nz = nx, ny, nz
        self.offsets = [(0, 0, 0)] + [(0, 0, k) for k in range(1, nz)]
        self.cell = {(0, 0): 0}
        for da in range(-1, 2):
            for db in range(-1, 2):
                key = (da % nx, db % ny)
                if key not in self.cell:
                    self.cell[key] = len(self.offsets)
                    self.offsets.append((key[0], key[1], 0))
        self.count = len(self.offsets)

    def cell_slot(self, da, db):
        return self.cell[(da % self.nx, db % self.ny)]

    def opposite(self, slot):
        dx, dy, dz = self.offsets[slot]
        if dz:
            return (self.nz - dz) % self.nz
        return self.cell_slot(-dx, -dy)

    def device(self, slot):
        dx, dy, dz = self.offsets[slot]
        return (
            lax.rem(lax.axis_index("gx") + dx, self.nx),
            lax.rem(lax.axis_index("gy") + dy, self.ny),
            lax.rem(lax.axis_index("gz") + dz, self.nz),
        )


def greet(slots):
    barrier = pltpu.get_barrier_semaphore()
    for s in range(1, slots.count):
        pl.semaphore_signal(barrier, inc=1, device_id=slots.device(s), device_id_type=MESH)
    pl.semaphore_wait(barrier, slots.count - 1)


def gather_kernel(
    slots, sigma_ref, eps_ref, pos, vel, fold, mass, charge, species, feats, kinds, send, recv, send2, recv2
):
    blocks = species.shape[1]
    half = vel[...] + 0.5 * time_step * fold[...] * mass[...]
    feats[0, 0:3, :] = pos[...] + time_step * half
    feats[0, 3:4, :] = charge[...]
    which = species[...]
    sigma = jnp.zeros((1, blocks), jnp.float32)
    eps = jnp.zeros((1, blocks), jnp.float32)
    for k in range(sigma_ref.shape[0]):
        sigma = jnp.where(which == k, sigma_ref[k], sigma)
        eps = jnp.where(which == k, eps_ref[k], eps)
    kinds[0] = jnp.zeros(kinds.shape[1:], jnp.float32)
    kinds[0, 0:1, 0:blocks] = sigma
    kinds[0, 1:2, 0:blocks] = jnp.sqrt(eps)
    greet(slots)
    copies = []
    for s in range(1, slots.count):
        there = slots.opposite(s)
        for ref, ss, rs in ((kinds, send2, recv2), (feats, send, recv)):
            copy = pltpu.make_async_remote_copy(
                src_ref=ref.at[0],
                dst_ref=ref.at[there],
                send_sem=ss.at[s],
                recv_sem=rs.at[there],
                device_id=slots.device(s),
                device_id_type=MESH,
            )
            copy.start()
            copies.append(copy)
    for copy in copies:
        copy.wait()


def stay_rows(mig_block, shape, width):
    block_of = lax.broadcasted_iota(jnp.int32, shape, 1) // width
    gone = block_of == mig_block[0, 0]
    for q in range(1, mig_block.shape[1]):
        gone = gone | (block_of == mig_block[0, q])
    return jnp.where(gone, 0.0, 1.0)


def pair_kernel(
    slots, blocks, tower, plate, counts, kinds, mig_block, feats, excl, acc, pos_out, cell_table,
    made_a, made_b, tail_a, tail_b,
):
    width = excl.shape[-1]
    words = excl.shape[2]
    lanes8 = width // words
    last = tower.shape[1] - 1
    nx, ny, nz = slots.nx, slots.ny, slots.nz
    lx, ly = float(nx), float(ny)
    my_layer = lax.axis_index("gz")
    for o in range(9):
        cell_table[o] = slots.cell_slot(o // 3 - 1, o % 3 - 1)
    acc[...] = jnp.zeros(acc.shape, acc.dtype)
    pos_out[...] = feats[0, 0:3, :] * stay_rows(mig_block, pos_out.shape, width)
    count = counts[0]
    bit = jnp.left_shift(1, lax.broadcasted_iota(jnp.int32, (lanes8, width), 0))
    lane = lax.broadcasted_iota(jnp.int32, (lanes8, width), 1)
    sub = lax.broadcasted_iota(jnp.int32, (8, width), 0)
    shift_h = soft_core / (lx * lx)
    edge = (cutoff_sq + soft_core) / (lx * lx)
    ratio = (ly / lx) ** 2
    scale = lx * lx / (cutoff_sq * cutoff_sq)
    units = (1.0 / lx, 1.0 / ly, 1.0 / lx)
    lengths = (lx, ly, lx)

    def three(row):
        value = jnp.broadcast_to(row, (8, width))
        high = value.astype(jnp.bfloat16).astype(jnp.float32)
        rest = value - high
        mid = rest.astype(jnp.bfloat16).astype(jnp.float32)
        return [high, mid, rest - mid]

    def by_row(values):
        made = jnp.zeros((8, width), jnp.float32)
        for i, v in enumerate(values):
            made = jnp.where(sub == i, v, made)
        return made

    def place(k):
        k = jnp.clip(k, 0, last)
        t = tower[0, k]
        p = plate[0, k]
        t_layer = lax.div(t, blocks)
        t_slot = t_layer - my_layer
        t_slot = jnp.where(t_slot < 0, t_slot + nz, t_slot)
        p_cell = lax.div(p, blocks)
        return t_slot, t - t_layer * blocks, cell_table[p_cell], p - p_cell * blocks

    def prepare(k, made):
        t_slot, t_block, p_slot, p_block = place(k)
        live = jnp.where(k < count, jnp.float32(1.0), jnp.float32(0.0))
        rows = feats[t_slot, :, pl.ds(pl.multiple_of(t_block * width, width), width)]
        prow = feats[p_slot, :, pl.ds(pl.multiple_of(p_block * width, width), width)]
        left, right = [], []
        for r in range(3):
            left.append(by_row([-v for v in three(prow[r : r + 1] * units[r])] + [1.0, 1.0, 1.0]))
            right.append(by_row([1.0, 1.0, 1.0] + three(rows[r : r + 1] * units[r])))
        high, mid, low = three(prow[3:4])
        left.append(by_row([high, high, high, mid, mid, low]))
        high, mid, low = three(rows[3:4] * (coulomb_k * scale / lx) * live)
        right.append(by_row([high, mid, low, high, mid, high]))
        zero = jnp.zeros((8, width), jnp.float32)
        left = jnp.concatenate(left, axis=0).T.astype(jnp.bfloat16)
        right = jnp.concatenate(
            [jnp.concatenate([right[r] if r == m else zero for r in range(4)], axis=0) for m in range(4)], axis=1
        ).astype(jnp.bfloat16)
        made[...] = jnp.dot(left, right, preferred_element_type=jnp.float32)

    def arithmetic(k, made, tail):
        t_slot, t_block, p_slot, p_block = place(k)
        safe = jnp.minimum(k, last)
        sig = 0.5 * (kinds[t_slot, 0, t_block] + kinds[p_slot, 0, p_block])
        depth = kinds[t_slot, 1, t_block] * kinds[p_slot, 1, p_block]
        sig2 = sig * sig
        sig6 = sig2 * sig2 * sig2
        live = jnp.where(k < count, jnp.float32(1.0), jnp.float32(0.0))
        att = (6.0 * scale / lx**6) * depth * sig6 * live
        rep = (12.0 * scale / lx**12) * depth * sig6 * sig6 * live
        sums = [None, None, None]
        for w in range(words):
            at = slice(w * lanes8, (w + 1) * lanes8)
            dx = made[at, 0:width]
            dy = made[at, width : 2 * width]
            dz = made[at, 2 * width : 3 * width]
            dx = dx - jnp.floor(dx + 0.5)
            dy = dy - jnp.floor(dy + 0.5)
            h = (dx * dx + dz * dz) + (ratio * (dy * dy) + shift_h)
            q = lax.rsqrt(h)
            f = jnp.maximum(edge - h, 0.0)
            s = q * q
            s3 = s * s * s
            g = f * f * s
            e = s3 * (rep * s3 - att) + made[at, 3 * width : 4 * width] * q
            c = jnp.where((excl[0, safe, w : w + 1, :] & bit) == 0, e * g, 0.0)
            parts = (c * dx, c * dy, c * dz)
            sums = [v if u is None else u + v for u, v in zip(sums, parts)]
            rx, ry, rz = [jnp.sum(v, axis=1, keepdims=True) for v in parts]
            tail[at, :] = jnp.where(lane == 0, rx, jnp.where(lane == 1, ry, rz))
        rows = [acc[t_slot, pl.ds(r * blocks + t_block, 1), :] for r in range(3)]
        for r in range(3):
            total = jnp.sum(sums[r], axis=0, keepdims=True) * lengths[r]
            acc[t_slot, pl.ds(r * blocks + t_block, 1), :] = rows[r] + total

    def finish(k, tail):
        t_slot, t_block, p_slot, p_block = place(k)
        on_plate = tail[...].T
        rows = [acc[p_slot, pl.ds(r * blocks + p_block, 1), :] for r in range(3)]
        for r in range(3):
            acc[p_slot, pl.ds(r * blocks + p_block, 1), :] = rows[r] - on_plate[r : r + 1] * lengths[r]

    tail_b[...] = jnp.zeros(tail_b.shape, jnp.float32)
    prepare(0, made_a)

    def step(i, carry):
        k = i * 2
        finish(k - 1, tail_b)
        prepare(k + 1, made_b)
        arithmetic(k, made_a, tail_a)
        finish(k, tail_a)
        prepare(k + 2, made_a)
        arithmetic(k + 1, made_b, tail_b)
        return carry

    steps = (count + 1) // 2
    lax.fori_loop(0, steps, step, 0)
    finish(2 * steps - 1, tail_b)


def return_kernel(
    slots, blocks, mig_block, mig_dest, acc, pos, vel, fold, mass,
    vel_full, force_out, arrived, landed, state, outgoing, send, recv, send2, recv2,
):
    atoms = pos.shape[1]
    width = atoms // blocks
    leaving = mig_block.shape[1]
    greet(slots)
    copies = []
    for s in range(1, slots.count):
        there = slots.opposite(s)
        copy = pltpu.make_async_remote_copy(
            src_ref=acc.at[s],
            dst_ref=landed.at[there],
            send_sem=send.at[s],
            recv_sem=recv.at[there],
            device_id=slots.device(s),
            device_id_type=MESH,
        )
        copy.start()
        copies.append(copy)
    half = vel[...] + 0.5 * time_step * fold[...] * mass[...]
    state[0:3, :] = pos[...] + time_step * half
    state[6:8, :] = jnp.zeros((2, atoms), jnp.float32)
    for copy in copies:
        copy.wait()
    force = acc[0]
    for s in range(1, slots.count):
        force = force + landed[s]
    for r in range(3):
        for b in range(blocks):
            force_out[r : r + 1, b * width : (b + 1) * width] = force[r * blocks + b : r * blocks + b + 1]
    full = half + 0.5 * time_step * force_out[...] * mass[...]
    state[3:6, :] = full
    for q in range(leaving):
        chosen = jnp.full((8, width), mig_block[0, q], jnp.int32)
        picked = jnp.zeros((8, width), jnp.float32)
        for b in range(blocks):
            picked = jnp.where(chosen == b, state[:, b * width : (b + 1) * width], picked)
        outgoing[0:6, q * width : (q + 1) * width] = picked[0:6]
        outgoing[6:8, q * width : (q + 1) * width] = jnp.full((2, width), mig_dest[0, q], jnp.int32).astype(
            jnp.float32
        )
    vel_full[...] = full
    arrived[0] = outgoing[...]
    near = sorted({slots.cell_slot(a, b) for a, b in source_offsets} - {0})
    for s in range(1, slots.nz):
        arrived[s] = jnp.zeros(arrived.shape[1:], jnp.float32)
    copies = []
    for s in near:
        there = slots.opposite(s)
        copy = pltpu.make_async_remote_copy(
            src_ref=outgoing,
            dst_ref=arrived.at[there],
            send_sem=send2.at[s],
            recv_sem=recv2.at[there],
            device_id=slots.device(s),
            device_id_type=MESH,
        )
        copy.start()
        copies.append(copy)
    for copy in copies:
        copy.wait()


def output_kernel(slots, blocks, mig_block, force, full, arrived, force_out, vel_out, arrive):
    width = force.shape[1] // blocks
    force_out[...] = force[...]
    vel_out[...] = full[...] * stay_rows(mig_block, full.shape, width)
    for i, (a, b) in enumerate(source_offsets):
        got = arrived[slots.cell_slot(a, b)]
        wanted = float((1 - a) * 3 + (1 - b))
        arrive[:, 0, i, :] = jnp.where(got[6:7] == wanted, got[0:6], 0.0)


def local(
    slots, positions, velocities, forces_old, inv_mass, charges, block_species, sigma_table, epsilon_table,
    tower_index, plate_index, tile_counts, exclusions, mig_block, mig_dest,
):
    atoms = positions.shape[1]
    blocks = block_species.shape[0]
    width = atoms // blocks
    n = slots.count
    leaving = mig_block.shape[1]
    vmem = pl.BlockSpec(memory_space=pltpu.VMEM)
    smem = pl.BlockSpec(memory_space=pltpu.SMEM)
    mass = inv_mass[None, :]
    f32 = jnp.float32
    lanes = max(width, blocks)
    sems = pltpu.SemaphoreType.DMA((n,))
    feats, kinds = pl.pallas_call(
        functools.partial(gather_kernel, slots),
        out_shape=(jax.ShapeDtypeStruct((n, 4, atoms), f32), jax.ShapeDtypeStruct((n, 2, lanes), f32)),
        in_specs=[smem, smem] + [vmem] * 6,
        out_specs=(vmem, vmem),
        scratch_shapes=[sems] * 4,
        compiler_params=pltpu.CompilerParams(collective_id=0, has_side_effects=True),
        name="gather_features",
    )(sigma_table, epsilon_table, positions, velocities, forces_old, mass, charges[None, :], block_species[None, :])
    rows = jax.ShapeDtypeStruct((3, atoms), f32)
    packed = jax.ShapeDtypeStruct((n, 3 * blocks, width), f32)
    acc, positions_new = pl.pallas_call(
        functools.partial(pair_kernel, slots, blocks),
        out_shape=(packed, rows),
        in_specs=[smem] * 5 + [vmem] * 2,
        out_specs=(vmem, vmem),
        scratch_shapes=[pltpu.SMEM((9,), jnp.int32)]
        + [pltpu.VMEM((width, 4 * width), f32)] * 2
        + [pltpu.VMEM((width, width), f32)] * 2,
        name="pair_forces",
    )(tower_index, plate_index, tile_counts, kinds, mig_block, feats, exclusions)
    strip = jax.ShapeDtypeStruct((n, 8, leaving * width), f32)
    full, force, arrived = pl.pallas_call(
        functools.partial(return_kernel, slots, blocks),
        out_shape=(rows, rows, strip),
        in_specs=[smem] * 2 + [vmem] * 5,
        out_specs=(vmem,) * 3,
        scratch_shapes=[
            pltpu.VMEM(packed.shape, f32),
            pltpu.VMEM((8, atoms), f32),
            pltpu.VMEM((8, leaving * width), f32),
        ]
        + [sems] * 4,
        compiler_params=pltpu.CompilerParams(collective_id=1, has_side_effects=True),
        name="return_forces",
    )(mig_block, mig_dest, acc, positions, velocities, forces_old, mass)
    forces_new, velocities_new, arrivals = pl.pallas_call(
        functools.partial(output_kernel, slots, blocks),
        out_shape=(rows, rows, jax.ShapeDtypeStruct((6, 1, len(source_offsets), leaving * width), f32)),
        in_specs=[smem] + [vmem] * 3,
        out_specs=(vmem,) * 3,
        name="outputs",
    )(mig_block, force, full, arrived)
    return positions_new, velocities_new, forces_new, arrivals


def solution(mesh):
    cells = ("gx", "gy", "gz")
    slots = Slots(mesh.shape["gx"], mesh.shape["gy"], mesh.shape["gz"])
    row = P(None, cells)
    flat = P(cells)
    pair = P(cells, None)
    in_specs = (
        row, row, row, flat, flat, flat, P(), P(), pair, pair, flat, P(cells, None, None, None), pair, pair,
    )
    out_specs = (row, row, row, P(None, cells, None, None))
    return jax.shard_map(
        functools.partial(local, slots), mesh=mesh, in_specs=in_specs, out_specs=out_specs, check_vma=False
    )
```

```python
import functools
import jax
import jax.numpy as jnp
from jax import lax
from jax.experimental import pallas as pl
from jax.experimental.pallas import tpu as pltpu
from jax.sharding import PartitionSpec as P

time_step = 0.2
soft_core = 0.09
cutoff_sq = 1.44
coulomb_k = 0.5
MESH = pl.DeviceIdType.MESH
UNROLL = 4
source_offsets = ((-1, -1), (-1, 0), (-1, 1), (0, -1), (0, 1), (1, -1), (1, 0), (1, 1))


class Slots:
    def __init__(self, nx, ny, nz):
        self.nx, self.ny, self.nz = nx, ny, nz
        self.offsets = [(0, 0, 0)] + [(0, 0, k) for k in range(1, nz)]
        self.cell = {(0, 0): 0}
        for da in range(-1, 2):
            for db in range(-1, 2):
                key = (da % nx, db % ny)
                if key not in self.cell:
                    self.cell[key] = len(self.offsets)
                    self.offsets.append((key[0], key[1], 0))
        self.count = len(self.offsets)

    def cell_slot(self, da, db):
        return self.cell[(da % self.nx, db % self.ny)]

    def opposite(self, slot):
        dx, dy, dz = self.offsets[slot]
        if dz:
            return (self.nz - dz) % self.nz
        return self.cell_slot(-dx, -dy)

    def device(self, slot):
        dx, dy, dz = self.offsets[slot]
        return (
            lax.rem(lax.axis_index("gx") + dx, self.nx),
            lax.rem(lax.axis_index("gy") + dy, self.ny),
            lax.rem(lax.axis_index("gz") + dz, self.nz),
        )


def greet(slots):
    barrier = pltpu.get_barrier_semaphore()
    for s in range(1, slots.count):
        pl.semaphore_signal(barrier, inc=1, device_id=slots.device(s), device_id_type=MESH)
    pl.semaphore_wait(barrier, slots.count - 1)


def gather_kernel(
    slots, sigma_ref, eps_ref, pos, vel, fold, mass, charge, species, feats, kinds, send, recv, send2, recv2
):
    blocks = species.shape[1]
    half = vel[...] + 0.5 * time_step * fold[...] * mass[...]
    feats[0, 0:3, :] = pos[...] + time_step * half
    feats[0, 3:4, :] = charge[...]
    which = species[...]
    sigma = jnp.zeros((1, blocks), jnp.float32)
    eps = jnp.zeros((1, blocks), jnp.float32)
    for k in range(sigma_ref.shape[0]):
        sigma = jnp.where(which == k, sigma_ref[k], sigma)
        eps = jnp.where(which == k, eps_ref[k], eps)
    kinds[0] = jnp.zeros(kinds.shape[1:], jnp.float32)
    kinds[0, 0:1, 0:blocks] = sigma
    kinds[0, 1:2, 0:blocks] = jnp.sqrt(eps)
    greet(slots)
    copies = []
    for s in range(1, slots.count):
        there = slots.opposite(s)
        for ref, ss, rs in ((kinds, send2, recv2), (feats, send, recv)):
            copy = pltpu.make_async_remote_copy(
                src_ref=ref.at[0],
                dst_ref=ref.at[there],
                send_sem=ss.at[s],
                recv_sem=rs.at[there],
                device_id=slots.device(s),
                device_id_type=MESH,
            )
            copy.start()
            copies.append(copy)
    for copy in copies:
        copy.wait()


def stay_rows(mig_block, shape, width):
    block_of = lax.broadcasted_iota(jnp.int32, shape, 1) // width
    gone = block_of == mig_block[0, 0]
    for q in range(1, mig_block.shape[1]):
        gone = gone | (block_of == mig_block[0, q])
    return jnp.where(gone, 0.0, 1.0)


def pair_kernel(
    slots, blocks, tower, plate, counts, kinds, mig_block, feats, excl, acc, pos_out, cell_table,
    made_a, made_b, tail_a, tail_b,
):
    width = excl.shape[-1]
    words = excl.shape[2]
    lanes8 = width // words
    last = tower.shape[1] - 1
    nx, ny, nz = slots.nx, slots.ny, slots.nz
    lx, ly = float(nx), float(ny)
    my_layer = lax.axis_index("gz")
    for o in range(9):
        cell_table[o] = slots.cell_slot(o // 3 - 1, o % 3 - 1)
    acc[...] = jnp.zeros(acc.shape, acc.dtype)
    pos_out[...] = feats[0, 0:3, :] * stay_rows(mig_block, pos_out.shape, width)
    count = counts[0]
    bit = jnp.left_shift(1, lax.broadcasted_iota(jnp.int32, (lanes8, width), 0))
    lane = lax.broadcasted_iota(jnp.int32, (lanes8, width), 1)
    sub = lax.broadcasted_iota(jnp.int32, (8, width), 0)
    shift_h = soft_core / (lx * lx)
    edge = (cutoff_sq + soft_core) / (lx * lx)
    ratio = (ly / lx) ** 2
    scale = lx * lx / (cutoff_sq * cutoff_sq)
    units = (1.0 / lx, 1.0 / ly, 1.0 / lx)
    lengths = (lx, ly, lx)

    def three(row):
        value = jnp.broadcast_to(row, (8, width))
        high = value.astype(jnp.bfloat16).astype(jnp.float32)
        rest = value - high
        mid = rest.astype(jnp.bfloat16).astype(jnp.float32)
        return [high, mid, rest - mid]

    def by_row(values):
        made = jnp.zeros((8, width), jnp.float32)
        for i, v in enumerate(values):
            made = jnp.where(sub == i, v, made)
        return made

    def place(k):
        k = jnp.clip(k, 0, last)
        t = tower[0, k]
        p = plate[0, k]
        t_layer = lax.div(t, blocks)
        t_slot = t_layer - my_layer
        t_slot = jnp.where(t_slot < 0, t_slot + nz, t_slot)
        p_cell = lax.div(p, blocks)
        return t_slot, t - t_layer * blocks, cell_table[p_cell], p - p_cell * blocks

    def prepare(k, made):
        t_slot, t_block, p_slot, p_block = place(k)
        live = jnp.where(k < count, jnp.float32(1.0), jnp.float32(0.0))
        rows = feats[t_slot, :, pl.ds(pl.multiple_of(t_block * width, width), width)]
        prow = feats[p_slot, :, pl.ds(pl.multiple_of(p_block * width, width), width)]
        left, right = [], []
        for r in range(3):
            left.append(by_row([-v for v in three(prow[r : r + 1] * units[r])] + [1.0, 1.0, 1.0]))
            right.append(by_row([1.0, 1.0, 1.0] + three(rows[r : r + 1] * units[r])))
        high, mid, low = three(prow[3:4])
        left.append(by_row([high, high, high, mid, mid, low]))
        high, mid, low = three(rows[3:4] * (coulomb_k * scale / lx) * live)
        right.append(by_row([high, mid, low, high, mid, high]))
        zero = jnp.zeros((8, width), jnp.float32)
        left = jnp.concatenate(left, axis=0).T.astype(jnp.bfloat16)
        right = jnp.concatenate(
            [jnp.concatenate([right[r] if r == m else zero for r in range(4)], axis=0) for m in range(4)], axis=1
        ).astype(jnp.bfloat16)
        made[...] = jnp.dot(left, right, preferred_element_type=jnp.float32)

    def arithmetic(k, made, tail):
        t_slot, t_block, p_slot, p_block = place(k)
        safe = jnp.minimum(k, last)
        sig = 0.5 * (kinds[t_slot, 0, t_block] + kinds[p_slot, 0, p_block])
        depth = kinds[t_slot, 1, t_block] * kinds[p_slot, 1, p_block]
        sig2 = sig * sig
        sig6 = sig2 * sig2 * sig2
        live = jnp.where(k < count, jnp.float32(1.0), jnp.float32(0.0))
        att = (6.0 * scale / lx**6) * depth * sig6 * live
        rep = (12.0 * scale / lx**12) * depth * sig6 * sig6 * live
        sums = [None, None, None]
        for w in range(words):
            at = slice(w * lanes8, (w + 1) * lanes8)
            dx = made[at, 0:width]
            dy = made[at, width : 2 * width]
            dz = made[at, 2 * width : 3 * width]
            dx = dx - jnp.floor(dx + 0.5)
            dy = dy - jnp.floor(dy + 0.5)
            h = (dx * dx + dz * dz) + (ratio * (dy * dy) + shift_h)
            q = lax.rsqrt(h)
            f = jnp.maximum(edge - h, 0.0)
            s = q * q
            s3 = s * s * s
            fq = f * q
            g = fq * fq
            e = s3 * (rep * s3 - att) + made[at, 3 * width : 4 * width] * q
            c = jnp.where((excl[0, safe, w : w + 1, :] & bit) == 0, e * g, 0.0)
            parts = (c * dx, c * dy, c * dz)
            sums = [v if u is None else u + v for u, v in zip(sums, parts)]
            for r in range(3):
                tail[r, at, :] = parts[r]
        rows = [acc[t_slot, pl.ds(r * blocks + t_block, 1), :] for r in range(3)]
        for r in range(3):
            total = jnp.sum(sums[r], axis=0, keepdims=True) * lengths[r]
            acc[t_slot, pl.ds(r * blocks + t_block, 1), :] = rows[r] + total

    def finish(k, tail):
        t_slot, t_block, p_slot, p_block = place(k)
        back = []
        for w in range(words):
            at = slice(w * lanes8, (w + 1) * lanes8)
            rx, ry, rz = [jnp.sum(tail[r, at, :], axis=1, keepdims=True) for r in range(3)]
            back.append(jnp.where(lane == 0, rx, jnp.where(lane == 1, ry, rz)))
        on_plate = jnp.concatenate(back, axis=0).T
        rows = [acc[p_slot, pl.ds(r * blocks + p_block, 1), :] for r in range(3)]
        for r in range(3):
            acc[p_slot, pl.ds(r * blocks + p_block, 1), :] = rows[r] - on_plate[r : r + 1] * lengths[r]

    tail_b[...] = jnp.zeros(tail_b.shape, jnp.float32)
    prepare(0, made_a)

    def step(i, carry):
        for half in range(UNROLL // 2):
            k = i * UNROLL + 2 * half
            finish(k - 1, tail_b)
            prepare(k + 1, made_b)
            arithmetic(k, made_a, tail_a)
            finish(k, tail_a)
            prepare(k + 2, made_a)
            arithmetic(k + 1, made_b, tail_b)
        return carry

    steps = (count + UNROLL - 1) // UNROLL
    lax.fori_loop(0, steps, step, 0)
    finish(UNROLL * steps - 1, tail_b)


def return_kernel(
    slots, blocks, mig_block, mig_dest, acc, pos, vel, fold, mass,
    vel_full, force_out, arrived, landed, state, outgoing, send, recv, send2, recv2,
):
    atoms = pos.shape[1]
    width = atoms // blocks
    leaving = mig_block.shape[1]
    greet(slots)
    copies = []
    for s in range(1, slots.count):
        there = slots.opposite(s)
        copy = pltpu.make_async_remote_copy(
            src_ref=acc.at[s],
            dst_ref=landed.at[there],
            send_sem=send.at[s],
            recv_sem=recv.at[there],
            device_id=slots.device(s),
            device_id_type=MESH,
        )
        copy.start()
        copies.append(copy)
    half = vel[...] + 0.5 * time_step * fold[...] * mass[...]
    state[0:3, :] = pos[...] + time_step * half
    state[6:8, :] = jnp.zeros((2, atoms), jnp.float32)
    for copy in copies:
        copy.wait()
    force = acc[0]
    for s in range(1, slots.count):
        force = force + landed[s]
    for r in range(3):
        for b in range(blocks):
            force_out[r : r + 1, b * width : (b + 1) * width] = force[r * blocks + b : r * blocks + b + 1]
    full = half + 0.5 * time_step * force_out[...] * mass[...]
    state[3:6, :] = full
    for q in range(leaving):
        chosen = jnp.full((8, width), mig_block[0, q], jnp.int32)
        picked = jnp.zeros((8, width), jnp.float32)
        for b in range(blocks):
            picked = jnp.where(chosen == b, state[:, b * width : (b + 1) * width], picked)
        outgoing[0:6, q * width : (q + 1) * width] = picked[0:6]
        outgoing[6:8, q * width : (q + 1) * width] = jnp.full((2, width), mig_dest[0, q], jnp.int32).astype(
            jnp.float32
        )
    vel_full[...] = full
    arrived[0] = outgoing[...]
    near = sorted({slots.cell_slot(a, b) for a, b in source_offsets} - {0})
    for s in range(1, slots.nz):
        arrived[s] = jnp.zeros(arrived.shape[1:], jnp.float32)
    copies = []
    for s in near:
        there = slots.opposite(s)
        copy = pltpu.make_async_remote_copy(
            src_ref=outgoing,
            dst_ref=arrived.at[there],
            send_sem=send2.at[s],
            recv_sem=recv2.at[there],
            device_id=slots.device(s),
            device_id_type=MESH,
        )
        copy.start()
        copies.append(copy)
    for copy in copies:
        copy.wait()


def output_kernel(slots, blocks, mig_block, force, full, arrived, force_out, vel_out, arrive):
    width = force.shape[1] // blocks
    force_out[...] = force[...]
    vel_out[...] = full[...] * stay_rows(mig_block, full.shape, width)
    for i, (a, b) in enumerate(source_offsets):
        got = arrived[slots.cell_slot(a, b)]
        wanted = float((1 - a) * 3 + (1 - b))
        arrive[:, 0, i, :] = jnp.where(got[6:7] == wanted, got[0:6], 0.0)


def local(
    slots, positions, velocities, forces_old, inv_mass, charges, block_species, sigma_table, epsilon_table,
    tower_index, plate_index, tile_counts, exclusions, mig_block, mig_dest,
):
    atoms = positions.shape[1]
    blocks = block_species.shape[0]
    width = atoms // blocks
    n = slots.count
    leaving = mig_block.shape[1]
    vmem = pl.BlockSpec(memory_space=pltpu.VMEM)
    smem = pl.BlockSpec(memory_space=pltpu.SMEM)
    mass = inv_mass[None, :]
    f32 = jnp.float32
    lanes = max(width, blocks)
    sems = pltpu.SemaphoreType.DMA((n,))
    feats, kinds = pl.pallas_call(
        functools.partial(gather_kernel, slots),
        out_shape=(jax.ShapeDtypeStruct((n, 4, atoms), f32), jax.ShapeDtypeStruct((n, 2, lanes), f32)),
        in_specs=[smem, smem] + [vmem] * 6,
        out_specs=(vmem, vmem),
        scratch_shapes=[sems] * 4,
        compiler_params=pltpu.CompilerParams(collective_id=0, has_side_effects=True),
        name="gather_features",
    )(sigma_table, epsilon_table, positions, velocities, forces_old, mass, charges[None, :], block_species[None, :])
    rows = jax.ShapeDtypeStruct((3, atoms), f32)
    packed = jax.ShapeDtypeStruct((n, 3 * blocks, width), f32)
    acc, positions_new = pl.pallas_call(
        functools.partial(pair_kernel, slots, blocks),
        out_shape=(packed, rows),
        in_specs=[smem] * 5 + [vmem] * 2,
        out_specs=(vmem, vmem),
        scratch_shapes=[pltpu.SMEM((9,), jnp.int32)]
        + [pltpu.VMEM((width, 4 * width), f32)] * 2
        + [pltpu.VMEM((3, width, width), f32)] * 2,
        name="pair_forces",
    )(tower_index, plate_index, tile_counts, kinds, mig_block, feats, exclusions)
    strip = jax.ShapeDtypeStruct((n, 8, leaving * width), f32)
    full, force, arrived = pl.pallas_call(
        functools.partial(return_kernel, slots, blocks),
        out_shape=(rows, rows, strip),
        in_specs=[smem] * 2 + [vmem] * 5,
        out_specs=(vmem,) * 3,
        scratch_shapes=[
            pltpu.VMEM(packed.shape, f32),
            pltpu.VMEM((8, atoms), f32),
            pltpu.VMEM((8, leaving * width), f32),
        ]
        + [sems] * 4,
        compiler_params=pltpu.CompilerParams(collective_id=1, has_side_effects=True),
        name="return_forces",
    )(mig_block, mig_dest, acc, positions, velocities, forces_old, mass)
    forces_new, velocities_new, arrivals = pl.pallas_call(
        functools.partial(output_kernel, slots, blocks),
        out_shape=(rows, rows, jax.ShapeDtypeStruct((6, 1, len(source_offsets), leaving * width), f32)),
        in_specs=[smem] + [vmem] * 3,
        out_specs=(vmem,) * 3,
        name="outputs",
    )(mig_block, force, full, arrived)
    return positions_new, velocities_new, forces_new, arrivals


def solution(mesh):
    cells = ("gx", "gy", "gz")
    slots = Slots(mesh.shape["gx"], mesh.shape["gy"], mesh.shape["gz"])
    row = P(None, cells)
    flat = P(cells)
    pair = P(cells, None)
    in_specs = (
        row, row, row, flat, flat, flat, P(), P(), pair, pair, flat, P(cells, None, None, None), pair, pair,
    )
    out_specs = (row, row, row, P(None, cells, None, None))
    return jax.shard_map(
        functools.partial(local, slots), mesh=mesh, in_specs=in_specs, out_specs=out_specs, check_vma=False
    )
```

```python
import functools
import jax
import jax.numpy as jnp
from jax import lax
from jax.experimental import pallas as pl
from jax.experimental.pallas import tpu as pltpu
from jax.sharding import PartitionSpec as P

time_step = 0.2
soft_core = 0.09
cutoff_sq = 1.44
coulomb_k = 0.5
MESH = pl.DeviceIdType.MESH
UNROLL = 4
source_offsets = ((-1, -1), (-1, 0), (-1, 1), (0, -1), (0, 1), (1, -1), (1, 0), (1, 1))


class Slots:
    def __init__(self, nx, ny, nz):
        self.nx, self.ny, self.nz = nx, ny, nz
        self.offsets = [(0, 0, 0)] + [(0, 0, k) for k in range(1, nz)]
        self.cell = {(0, 0): 0}
        for da in range(-1, 2):
            for db in range(-1, 2):
                key = (da % nx, db % ny)
                if key not in self.cell:
                    self.cell[key] = len(self.offsets)
                    self.offsets.append((key[0], key[1], 0))
        self.count = len(self.offsets)

    def cell_slot(self, da, db):
        return self.cell[(da % self.nx, db % self.ny)]

    def opposite(self, slot):
        dx, dy, dz = self.offsets[slot]
        if dz:
            return (self.nz - dz) % self.nz
        return self.cell_slot(-dx, -dy)

    def device(self, slot):
        dx, dy, dz = self.offsets[slot]
        return (
            lax.rem(lax.axis_index("gx") + dx, self.nx),
            lax.rem(lax.axis_index("gy") + dy, self.ny),
            lax.rem(lax.axis_index("gz") + dz, self.nz),
        )


def greet(slots):
    barrier = pltpu.get_barrier_semaphore()
    for s in range(1, slots.count):
        pl.semaphore_signal(barrier, inc=1, device_id=slots.device(s), device_id_type=MESH)
    pl.semaphore_wait(barrier, slots.count - 1)


def gather_kernel(
    slots, sigma_ref, eps_ref, pos, vel, fold, mass, charge, species, feats, kinds, send, recv, send2, recv2
):
    blocks = species.shape[1]
    half = vel[...] + 0.5 * time_step * fold[...] * mass[...]
    feats[0, 0:3, :] = pos[...] + time_step * half
    feats[0, 3:4, :] = charge[...]
    which = species[...]
    sigma = jnp.zeros((1, blocks), jnp.float32)
    eps = jnp.zeros((1, blocks), jnp.float32)
    for k in range(sigma_ref.shape[0]):
        sigma = jnp.where(which == k, sigma_ref[k], sigma)
        eps = jnp.where(which == k, eps_ref[k], eps)
    kinds[0] = jnp.zeros(kinds.shape[1:], jnp.float32)
    kinds[0, 0:1, 0:blocks] = sigma
    kinds[0, 1:2, 0:blocks] = jnp.sqrt(eps)
    greet(slots)
    copies = []

    def send_to(slot, target, there):
        for ref, ss, rs in ((kinds, send2, recv2), (feats, send, recv)):
            copy = pltpu.make_async_remote_copy(
                src_ref=ref.at[slot],
                dst_ref=ref.at[there],
                send_sem=ss.at[there],
                recv_sem=rs.at[there],
                device_id=slots.device(target),
                device_id_type=MESH,
            )
            copy.start()
            copies.append(copy)

    across = slots.cell_slot(0, 1) if slots.ny == 2 else 0
    relayed = []
    for s in range(slots.count - 1, 0, -1):
        dx, dy, dz = slots.offsets[s]
        if across and dx and dy:
            relayed.append((slots.cell_slot(dx, 0), s))
        else:
            send_to(0, s, slots.opposite(s))
    direct = list(copies)
    arrivals_of = {}
    for copy, s in zip(direct, [t for t in range(slots.count - 1, 0, -1) if t not in [r for _, r in relayed] for _ in (0, 1)]):
        arrivals_of.setdefault(slots.opposite(s), []).append(copy)
    for held, there in relayed:
        for copy in arrivals_of[held]:
            copy.wait_recv()
        send_to(held, across, there)
    early = [copy for held, _ in relayed for copy in arrivals_of[held]]
    for copy in copies:
        copy.wait_send()
        if not any(copy is e for e in early):
            copy.wait_recv()


def stay_rows(mig_block, shape, width):
    block_of = lax.broadcasted_iota(jnp.int32, shape, 1) // width
    gone = block_of == mig_block[0, 0]
    for q in range(1, mig_block.shape[1]):
        gone = gone | (block_of == mig_block[0, q])
    return jnp.where(gone, 0.0, 1.0)


def pair_kernel(
    slots, blocks, tower, plate, counts, kinds, mig_block, feats, excl, acc, pos_out, cell_table,
    made_a, made_b, tail_a, tail_b,
):
    width = excl.shape[-1]
    words = excl.shape[2]
    lanes8 = width // words
    last = tower.shape[1] - 1
    nx, ny, nz = slots.nx, slots.ny, slots.nz
    lx, ly = float(nx), float(ny)
    my_layer = lax.axis_index("gz")
    for o in range(9):
        cell_table[o] = slots.cell_slot(o // 3 - 1, o % 3 - 1)
    acc[...] = jnp.zeros(acc.shape, acc.dtype)
    pos_out[...] = feats[0, 0:3, :] * stay_rows(mig_block, pos_out.shape, width)
    count = counts[0]
    bit = jnp.left_shift(1, lax.broadcasted_iota(jnp.int32, (lanes8, width), 0))
    lane = lax.broadcasted_iota(jnp.int32, (lanes8, width), 1)
    sub = lax.broadcasted_iota(jnp.int32, (8, width), 0)
    shift_h = soft_core / (lx * lx)
    edge = (cutoff_sq + soft_core) / (lx * lx)
    ratio = (ly / lx) ** 2
    scale = lx * lx / (cutoff_sq * cutoff_sq)
    units = (1.0 / lx, 1.0 / ly, 1.0 / lx)
    lengths = (lx, ly, lx)

    def three(row):
        value = jnp.broadcast_to(row, (8, width))
        high = value.astype(jnp.bfloat16).astype(jnp.float32)
        rest = value - high
        mid = rest.astype(jnp.bfloat16).astype(jnp.float32)
        return [high, mid, rest - mid]

    def by_row(values):
        made = jnp.zeros((8, width), jnp.float32)
        for i, v in enumerate(values):
            made = jnp.where(sub == i, v, made)
        return made

    def place(k):
        k = jnp.clip(k, 0, last)
        t = tower[0, k]
        p = plate[0, k]
        t_layer = lax.div(t, blocks)
        t_slot = t_layer - my_layer
        t_slot = jnp.where(t_slot < 0, t_slot + nz, t_slot)
        p_cell = lax.div(p, blocks)
        return t_slot, t - t_layer * blocks, cell_table[p_cell], p - p_cell * blocks

    def prepare(k, made):
        t_slot, t_block, p_slot, p_block = place(k)
        live = jnp.where(k < count, jnp.float32(1.0), jnp.float32(0.0))
        rows = feats[t_slot, :, pl.ds(pl.multiple_of(t_block * width, width), width)]
        prow = feats[p_slot, :, pl.ds(pl.multiple_of(p_block * width, width), width)]
        left, right = [], []
        for r in range(3):
            left.append(by_row([-v for v in three(prow[r : r + 1] * units[r])] + [1.0, 1.0, 1.0]))
            right.append(by_row([1.0, 1.0, 1.0] + three(rows[r : r + 1] * units[r])))
        high, mid, low = three(prow[3:4])
        left.append(by_row([high, high, high, mid, mid, low]))
        high, mid, low = three(rows[3:4] * (coulomb_k * scale / lx) * live)
        right.append(by_row([high, mid, low, high, mid, high]))
        zero = jnp.zeros((8, width), jnp.float32)
        left = jnp.concatenate(left, axis=0).T.astype(jnp.bfloat16)
        right = jnp.concatenate(
            [jnp.concatenate([right[r] if r == m else zero for r in range(4)], axis=0) for m in range(4)], axis=1
        ).astype(jnp.bfloat16)
        made[...] = jnp.dot(left, right, preferred_element_type=jnp.float32)

    def arithmetic(k, made, tail):
        t_slot, t_block, p_slot, p_block = place(k)
        safe = jnp.minimum(k, last)
        sig = 0.5 * (kinds[t_slot, 0, t_block] + kinds[p_slot, 0, p_block])
        depth = kinds[t_slot, 1, t_block] * kinds[p_slot, 1, p_block]
        sig2 = sig * sig
        sig6 = sig2 * sig2 * sig2
        live = jnp.where(k < count, jnp.float32(1.0), jnp.float32(0.0))
        att = (6.0 * scale / lx**6) * depth * sig6 * live
        rep = (12.0 * scale / lx**12) * depth * sig6 * sig6 * live
        sums = [None, None, None]
        for w in range(words):
            at = slice(w * lanes8, (w + 1) * lanes8)
            dx = made[at, 0:width]
            dy = made[at, width : 2 * width]
            dz = made[at, 2 * width : 3 * width]
            dx = dx - jnp.floor(dx + 0.5)
            dy = dy - jnp.floor(dy + 0.5)
            h = (dx * dx + dz * dz) + (ratio * (dy * dy) + shift_h)
            q = lax.rsqrt(h)
            f = jnp.maximum(edge - h, 0.0)
            s = q * q
            s3 = s * s * s
            fq = f * q
            g = fq * fq
            e = s3 * (rep * s3 - att) + made[at, 3 * width : 4 * width] * q
            c = jnp.where((excl[0, safe, w : w + 1, :] & bit) == 0, e * g, 0.0)
            parts = (c * dx, c * dy, c * dz)
            sums = [v if u is None else u + v for u, v in zip(sums, parts)]
            for r in range(3):
                tail[r, at, :] = parts[r]
        rows = [acc[t_slot, pl.ds(r * blocks + t_block, 1), :] for r in range(3)]
        for r in range(3):
            total = jnp.sum(sums[r], axis=0, keepdims=True) * lengths[r]
            acc[t_slot, pl.ds(r * blocks + t_block, 1), :] = rows[r] + total

    def finish(k, tail):
        t_slot, t_block, p_slot, p_block = place(k)
        back = []
        for w in range(words):
            at = slice(w * lanes8, (w + 1) * lanes8)
            rx, ry, rz = [jnp.sum(tail[r, at, :], axis=1, keepdims=True) for r in range(3)]
            back.append(jnp.where(lane == 0, rx, jnp.where(lane == 1, ry, rz)))
        on_plate = jnp.concatenate(back, axis=0).T
        rows = [acc[p_slot, pl.ds(r * blocks + p_block, 1), :] for r in range(3)]
        for r in range(3):
            acc[p_slot, pl.ds(r * blocks + p_block, 1), :] = rows[r] - on_plate[r : r + 1] * lengths[r]

    tail_b[...] = jnp.zeros(tail_b.shape, jnp.float32)
    prepare(0, made_a)

    def step(i, carry):
        for half in range(UNROLL // 2):
            k = i * UNROLL + 2 * half
            finish(k - 1, tail_b)
            prepare(k + 1, made_b)
            arithmetic(k, made_a, tail_a)
            finish(k, tail_a)
            prepare(k + 2, made_a)
            arithmetic(k + 1, made_b, tail_b)
        return carry

    steps = (count + UNROLL - 1) // UNROLL
    lax.fori_loop(0, steps, step, 0)
    finish(UNROLL * steps - 1, tail_b)


def return_kernel(
    slots, blocks, mig_block, mig_dest, acc, pos, vel, fold, mass,
    vel_full, force_out, arrived, landed, state, outgoing, send, recv, send2, recv2,
):
    atoms = pos.shape[1]
    width = atoms // blocks
    leaving = mig_block.shape[1]
    greet(slots)
    copies = []
    for s in range(1, slots.count):
        there = slots.opposite(s)
        copy = pltpu.make_async_remote_copy(
            src_ref=acc.at[s],
            dst_ref=landed.at[there],
            send_sem=send.at[s],
            recv_sem=recv.at[there],
            device_id=slots.device(s),
            device_id_type=MESH,
        )
        copy.start()
        copies.append(copy)
    half = vel[...] + 0.5 * time_step * fold[...] * mass[...]
    state[0:3, :] = pos[...] + time_step * half
    state[6:8, :] = jnp.zeros((2, atoms), jnp.float32)
    for copy in copies:
        copy.wait()
    force = acc[0]
    for s in range(1, slots.count):
        force = force + landed[s]
    for r in range(3):
        for b in range(blocks):
            force_out[r : r + 1, b * width : (b + 1) * width] = force[r * blocks + b : r * blocks + b + 1]
    full = half + 0.5 * time_step * force_out[...] * mass[...]
    state[3:6, :] = full
    for q in range(leaving):
        chosen = jnp.full((8, width), mig_block[0, q], jnp.int32)
        picked = jnp.zeros((8, width), jnp.float32)
        for b in range(blocks):
            picked = jnp.where(chosen == b, state[:, b * width : (b + 1) * width], picked)
        outgoing[0:6, q * width : (q + 1) * width] = picked[0:6]
        outgoing[6:8, q * width : (q + 1) * width] = jnp.full((2, width), mig_dest[0, q], jnp.int32).astype(
            jnp.float32
        )
    vel_full[...] = full
    arrived[0] = outgoing[...]
    near = sorted({slots.cell_slot(a, b) for a, b in source_offsets} - {0})
    for s in range(1, slots.nz):
        arrived[s] = jnp.zeros(arrived.shape[1:], jnp.float32)
    copies = []
    for s in near:
        there = slots.opposite(s)
        copy = pltpu.make_async_remote_copy(
            src_ref=outgoing,
            dst_ref=arrived.at[there],
            send_sem=send2.at[s],
            recv_sem=recv2.at[there],
            device_id=slots.device(s),
            device_id_type=MESH,
        )
        copy.start()
        copies.append(copy)
    for copy in copies:
        copy.wait()


def output_kernel(slots, blocks, mig_block, force, full, arrived, force_out, vel_out, arrive):
    width = force.shape[1] // blocks
    force_out[...] = force[...]
    vel_out[...] = full[...] * stay_rows(mig_block, full.shape, width)
    for i, (a, b) in enumerate(source_offsets):
        got = arrived[slots.cell_slot(a, b)]
        wanted = float((1 - a) * 3 + (1 - b))
        arrive[:, 0, i, :] = jnp.where(got[6:7] == wanted, got[0:6], 0.0)


def local(
    slots, positions, velocities, forces_old, inv_mass, charges, block_species, sigma_table, epsilon_table,
    tower_index, plate_index, tile_counts, exclusions, mig_block, mig_dest,
):
    atoms = positions.shape[1]
    blocks = block_species.shape[0]
    width = atoms // blocks
    n = slots.count
    leaving = mig_block.shape[1]
    vmem = pl.BlockSpec(memory_space=pltpu.VMEM)
    smem = pl.BlockSpec(memory_space=pltpu.SMEM)
    mass = inv_mass[None, :]
    f32 = jnp.float32
    lanes = max(width, blocks)
    sems = pltpu.SemaphoreType.DMA((n,))
    feats, kinds = pl.pallas_call(
        functools.partial(gather_kernel, slots),
        out_shape=(jax.ShapeDtypeStruct((n, 4, atoms), f32), jax.ShapeDtypeStruct((n, 2, lanes), f32)),
        in_specs=[smem, smem] + [vmem] * 6,
        out_specs=(vmem, vmem),
        scratch_shapes=[sems] * 4,
        compiler_params=pltpu.CompilerParams(collective_id=0, has_side_effects=True),
        name="gather_features",
    )(sigma_table, epsilon_table, positions, velocities, forces_old, mass, charges[None, :], block_species[None, :])
    rows = jax.ShapeDtypeStruct((3, atoms), f32)
    packed = jax.ShapeDtypeStruct((n, 3 * blocks, width), f32)
    acc, positions_new = pl.pallas_call(
        functools.partial(pair_kernel, slots, blocks),
        out_shape=(packed, rows),
        in_specs=[smem] * 5 + [vmem] * 2,
        out_specs=(vmem, vmem),
        scratch_shapes=[pltpu.SMEM((9,), jnp.int32)]
        + [pltpu.VMEM((width, 4 * width), f32)] * 2
        + [pltpu.VMEM((3, width, width), f32)] * 2,
        name="pair_forces",
    )(tower_index, plate_index, tile_counts, kinds, mig_block, feats, exclusions)
    strip = jax.ShapeDtypeStruct((n, 8, leaving * width), f32)
    full, force, arrived = pl.pallas_call(
        functools.partial(return_kernel, slots, blocks),
        out_shape=(rows, rows, strip),
        in_specs=[smem] * 2 + [vmem] * 5,
        out_specs=(vmem,) * 3,
        scratch_shapes=[
            pltpu.VMEM(packed.shape, f32),
            pltpu.VMEM((8, atoms), f32),
            pltpu.VMEM((8, leaving * width), f32),
        ]
        + [sems] * 4,
        compiler_params=pltpu.CompilerParams(collective_id=1, has_side_effects=True),
        name="return_forces",
    )(mig_block, mig_dest, acc, positions, velocities, forces_old, mass)
    forces_new, velocities_new, arrivals = pl.pallas_call(
        functools.partial(output_kernel, slots, blocks),
        out_shape=(rows, rows, jax.ShapeDtypeStruct((6, 1, len(source_offsets), leaving * width), f32)),
        in_specs=[smem] + [vmem] * 3,
        out_specs=(vmem,) * 3,
        name="outputs",
    )(mig_block, force, full, arrived)
    return positions_new, velocities_new, forces_new, arrivals


def solution(mesh):
    cells = ("gx", "gy", "gz")
    slots = Slots(mesh.shape["gx"], mesh.shape["gy"], mesh.shape["gz"])
    row = P(None, cells)
    flat = P(cells)
    pair = P(cells, None)
    in_specs = (
        row, row, row, flat, flat, flat, P(), P(), pair, pair, flat, P(cells, None, None, None), pair, pair,
    )
    out_specs = (row, row, row, P(None, cells, None, None))
    return jax.shard_map(
        functools.partial(local, slots), mesh=mesh, in_specs=in_specs, out_specs=out_specs, check_vma=False
    )
```
